256 devices in a mesh: tile: 32 (over x, y, core), comp: 8 (over z).
Axes of the slice: x: 4, y: 4, z: 8, core: 2. Of those that a mesh axis runs over, the one named last changes fastest.
Arguments:
- spectrum: float32 [1152, 262144], P('comp', 'tile'), may hold values from 0.05 to 1
- sea_mask: int32 [262144], P('tile'), may hold values 0 or 1
- wind_speed: float32 [262144], P(('tile', 'comp')), may hold values from 0.5 to 2
- wind_dir: float32 [262144], P(('tile', 'comp')), may hold values from -3.140625 to 3.140625
- dia_plus: int32 [1152], replicated, may hold values from 0 to 1151
- dia_minus: int32 [1152], replicated, may hold values from 0 to 1151
- farm_point: int32 [32, 8, 64], P('tile', 'comp'), may hold values from 0 to 1023, as said below
- farm_route: int32 [32, 8, 64, 1], P('tile', 'comp'), may hold values from 0 to 31; in each aligned block of 64 rows (0 to 63, 64 to 127, ..., all dimensions but the last counted through in order) at most 8 rows name the same one
- farm_matrix: bfloat16 [32, 36, 32, 32], P('tile')
Outputs:
- wave_spectrum: float32 [1152, 262144], P(None, ('tile', 'comp'))
The draws below stay inside these ranges and needn't reach their ends.
Inputs may be any that keep to these rules, and one draw needn't show every extreme that they name: `farm_point`: the 64 entries of one device's list are distinct. `farm_route`: no farm is named more than 8 times in one device's list.
All inputs are finite; a program needn't handle non-finite values. No bound on the sum of `sea_mask` on one device may be relied on, other than what follows from the above.
Results may differ from the reference program's by a relative error of at most 0.00051.
Values may be sent and summed in bfloat16 or wider, within the bound.
No kernel may reach another device: no remote copies, remote signals or barrier semaphores. Data moves between devices by JAX's collectives and lax.ppermute only.
A program may use at most 128 MiB of HBM per device.

```python
import math
import jax
import jax.numpy as jnp
import numpy as np
from jax import lax

NF = 36
ND = 32
NC = 1152
NY = 1024
PROP_STEPS = 2
FCAP = 64
CAP = 8
NX = 256
FARMS = 32
GROUPS = 8
TILE_PTS = 8192
DEV_PTS = 1024
NPTS = 262144


def draw_farm_point(key, part):
    keys = jax.random.split(key, FARMS * GROUPS)

    def pick_block(block_key, block):
        order = jax.random.permutation(block_key, DEV_PTS)[:FCAP].astype(jnp.int32)
        present = jnp.any(order == DEV_PTS - 1)
        forced = order.at[0].set(DEV_PTS - 1)
        return jnp.where((block == 0) & jnp.logical_not(present), forced, order)
    blocks = jax.vmap(pick_block)(keys, jnp.arange(FARMS * GROUPS, dtype=jnp.int32))
    return blocks.reshape(FARMS, GROUPS, FCAP).astype(jnp.int32)


def draw_farm_matrix(key, part):
    first_key, second_key = jax.random.split(key)
    dims = (FARMS, NF, ND, ND)
    spread = 0.35 * jax.random.normal(first_key, dims, jnp.float32) / math.sqrt(ND)
    keep = jax.random.uniform(second_key, dims, jnp.float32, 0.45, 0.75)
    diagonal = (jnp.arange(ND)[:, None] == jnp.arange(ND)[None, :]).astype(jnp.float32)
    return (spread + diagonal * keep).astype(jnp.bfloat16)


def touch_ends(values, rng, low, high):
    shape = values.shape
    spot = [jax.random.randint(jax.random.fold_in(rng, axis), (), 0, shape[axis]) for axis in range(len(shape))]
    values = values.at[tuple(spot)].set(low)
    longest = shape.index(max(shape))
    spot[longest] = (spot[longest] + 1) % shape[longest]
    return values.at[tuple(spot)].set(high)


def block_levels(own_key, extent, pieces, least, top_value):
    factor_of, own = 1.0, jax.random.fold_in(own_key, 6)
    for axis_at, shards_of in pieces:
        heights = jnp.exp(jax.random.uniform(jax.random.fold_in(own, axis_at), (shards_of,), jnp.float32, least / len(pieces), top_value / len(pieces)))
        factor_of = factor_of * jnp.repeat(heights, extent[axis_at] // shards_of).reshape([-1 if axis == axis_at else 1 for axis in range(len(extent))])
    return factor_of


def shared_out(key, own, number, rows, number_of, top, reach, slope):
    order = jax.random.permutation(key, number_of)
    crowded, usual = shares(number_of, rows * top, reach, slope, True), shares(number_of, rows * top, reach, slope, False)
    places = jnp.arange(number_of)

    def named(sizes, rotation):
        used = int((sizes > 0).sum())
        fixed = max(1, used // 4)
        shifted = fixed + (places - fixed + rotation * (used - fixed)) % max(1, number_of - fixed)
        return jnp.zeros((number_of,), jnp.int32).at[order[jnp.where(places < fixed, places, shifted)]].set(jnp.asarray(sizes, jnp.int32))

    sizes = jnp.where(number % 4 == 0, named(crowded, number // 4), named(usual, number - number // 4 - 1))
    mixed = jax.random.permutation(jax.random.fold_in(own, 3), number_of)
    source_of, receiver = mixed[0:number_of // 2 * 2:2], mixed[1:number_of // 2 * 2:2]
    margin = jnp.minimum(sizes[source_of] - 1, reach - sizes[receiver]) // 2
    margin = jnp.where((source_of == order[0]) | (receiver == order[0]) | (sizes[receiver] == 0), 0, jnp.maximum(margin, 0))
    shifted = jax.random.randint(jax.random.fold_in(own, 4), (number_of // 2,), 0, 1 << 20) % (margin + 1)
    sizes = sizes.at[source_of].add(-shifted).at[receiver].add(shifted)
    members = jnp.searchsorted(jnp.cumsum(sizes), jnp.arange(rows * top), side="right").astype(jnp.int32)
    grid = members.reshape(top, rows).T
    grid = grid[jax.random.permutation(jax.random.fold_in(own, 1), rows)]
    rotation = jax.random.randint(jax.random.fold_in(own, 2), (rows, 1), 0, top)
    return jnp.take_along_axis(grid, (jnp.arange(top)[None, :] + rotation) % top, axis=1)


def shares(count, total, limit, skew, full):
    weights = [(1 << 20) // math.isqrt(rank ** skew) + 1 for rank in range(1, count + 1)]
    largest = limit if full else min(limit, max(-(-total // count), total * weights[0] // sum(weights)))
    least = 1 if total - largest >= count - 1 else 0
    given, surplus = [largest] + [least] * (count - 1), total - largest - least * (count - 1)
    while surplus > 0:
        candidates = [i for i in range(1, count) if given[i] < largest] or [i for i in range(1, count) if given[i] < limit]
        mass, left = sum([weights[i] for i in candidates]), surplus
        for i in candidates:
            extra = min(limit - given[i], max(1, left * weights[i] // mass), surplus)
            given[i] = given[i] + extra
            surplus = surplus - extra
    return np.array(given)


def setup_inputs(seed: int = 0) -> dict:
    arg_keys = jax.random.split(jax.random.key(seed), 10)
    spectrum = jnp.clip(jnp.exp(math.log(1.0) - 2.9957323 * jax.random.uniform(arg_keys[0], (NC, NPTS), jnp.float32) ** block_levels(arg_keys[0], (NC, NPTS), ((0, 8), (1, 32)), -0.2, 0.2)), 0.05, 1.0)
    sea_mask = touch_ends((jax.random.randint(arg_keys[1], (NPTS,), 0, 10) < 9).astype(jnp.int32), jax.random.fold_in(arg_keys[1], 1), 0, 1)
    wind_speed = jnp.clip(0.5 + 1.5 * jax.random.uniform(arg_keys[2], (NPTS,), jnp.float32) ** block_levels(arg_keys[2], (NPTS,), ((0, 256),), -0.2, 0.2), 0.5, 2.0)
    wind_dir = jnp.clip(jax.random.uniform(arg_keys[3], (NPTS,), jnp.float32, -3.140625, 3.140625), -3.140625, 3.140625)
    dia_plus = touch_ends(jax.random.randint(arg_keys[4], (NC,), 0, NC), jax.random.fold_in(arg_keys[4], 1), 0, NC - 1).astype(jnp.int32)
    dia_minus = touch_ends(jax.random.randint(arg_keys[5], (NC,), 0, NC), jax.random.fold_in(arg_keys[5], 1), 0, NC - 1).astype(jnp.int32)
    farm_point = draw_farm_point(jax.random.fold_in(arg_keys[9], 71), 0)
    farm_route_keys = jax.random.split(jax.random.fold_in(arg_keys[7], 1), FARMS * GROUPS * FCAP // FCAP)
    farm_route_turns = jax.random.permutation(jax.random.fold_in(arg_keys[7], 3), FARMS * GROUPS * FCAP // FCAP)
    farm_route = jax.vmap(lambda own, number: shared_out(jax.random.fold_in(arg_keys[7], 2), own, number, FCAP, FARMS, 1, CAP, 2))(farm_route_keys, farm_route_turns).reshape((FARMS, GROUPS, FCAP, 1))
    farm_matrix = draw_farm_matrix(jax.random.fold_in(arg_keys[9], 71), 0)
    return {"spectrum": spectrum, "sea_mask": sea_mask, "wind_speed": wind_speed, "wind_dir": wind_dir, "dia_plus": dia_plus, "dia_minus": dia_minus, "farm_point": farm_point, "farm_route": farm_route, "farm_matrix": farm_matrix}


cfl_scale = 0.6
grow_rate = 0.35
break_rate = 0.6
pair_rate = 0.5


def component_tables(first, count):
    index = first + jnp.arange(count, dtype=jnp.int32)
    band = (index // ND).astype(jnp.float32)
    heading = 2.0 * math.pi * ((index % ND).astype(jnp.float32) + 0.5) / ND
    speed = cfl_scale / (1.0 + 0.1 * band)
    east = speed * jnp.cos(heading)
    north = speed * jnp.sin(heading)
    return band, heading, (jnp.maximum(east, 0.0), jnp.maximum(-east, 0.0), jnp.maximum(north, 0.0), jnp.maximum(-north, 0.0))


def advance(padded, coeffs):
    inner = padded[:, 1:-1]
    west = padded[:, :-2]
    eastward = padded[:, 2:]
    rows = jnp.pad(inner, ((0, 0), (0, 0), (1, 1)))
    south = rows[:, :, :-2]
    northward = rows[:, :, 2:]
    x_plus, x_minus, y_plus, y_minus = [term[:, None, None] for term in coeffs]
    return (inner - x_plus * (inner - west) - x_minus * (inner - eastward)
            - y_plus * (inner - south) - y_minus * (inner - northward))


def sources(field, speed, direction, dia_plus, dia_minus, band, heading):
    growth = grow_rate * speed[None, :] * jnp.maximum(jnp.cos(heading[:, None] - direction[None, :]), 0.0) * ((band[:, None] + 1.0) / NF)
    mean_energy = jnp.sum(field, axis=0, keepdims=True) / NC
    loss = break_rate * mean_energy * (0.5 + band[:, None] / NF)
    plus = jnp.take(field, dia_plus, axis=0)
    minus = jnp.take(field, dia_minus, axis=0)
    pairs = pair_rate * (field * field * (plus + minus) - 2.0 * field * plus * minus)
    return field + growth * field - loss * field + pairs


def reference(spectrum, sea_mask, wind_speed, wind_dir, dia_plus, dia_minus, farm_point, farm_route, farm_matrix):
    band, heading, coeffs = component_tables(0, NC)
    sea = sea_mask.reshape(NX, NY).astype(jnp.float32)
    banded = tuple(term.reshape(NF, ND) for term in coeffs)

    def band_step(items):
        field = items[0]
        terms = items[1:]
        for step in range(PROP_STEPS):
            padded = jnp.pad(field, ((0, 0), (1, 1), (0, 0)))
            field = advance(padded, terms) * sea[None]
        return field

    moved = lax.map(band_step, (spectrum.reshape(NF, ND, NX, NY),) + banded)
    tiles = moved.reshape(NC, FARMS, TILE_PTS).transpose(1, 0, 2)
    tables = farm_matrix.astype(jnp.float32)

    def tile_step(items):
        field, speed, direction, points, routes = items
        sourced = sources(field, speed, direction, dia_plus, dia_minus, band, heading)
        local = (jnp.arange(GROUPS, dtype=jnp.int32)[:, None] * DEV_PTS + points).reshape(-1)
        cells = jnp.take(sourced, local, axis=1).T.astype(jnp.bfloat16)
        chosen = tables[routes.reshape(-1)]
        farmed = jnp.einsum('sfde,sfe->sfd', chosen, cells.astype(jnp.float32).reshape(-1, NF, ND), precision=lax.Precision.HIGHEST)
        return sourced.at[:, local].set(farmed.reshape(-1, NC).T)

    result = lax.map(tile_step, (tiles, wind_speed.reshape(FARMS, TILE_PTS), wind_dir.reshape(FARMS, TILE_PTS), farm_point, farm_route.reshape(FARMS, GROUPS, FCAP)))
    return result.transpose(1, 0, 2).reshape(NC, NPTS)
```

```python
import functools
import math

import jax
import jax.numpy as jnp
from jax import lax
from jax.experimental import pallas as pl
from jax.experimental.pallas import tpu as pltpu
from jax.sharding import PartitionSpec as P

NF = 36
ND = 32
NC = 1152
NY = 1024
COLS = 8
PAIRS = 9
SLOTS = 64
GROUPS_F = 9
FARMS = 32
Q = 65535.0

cfl_scale = 0.6
grow_rate = 0.35
break_rate = 0.6
pair_rate = 0.5


COS = [math.cos(2.0 * math.pi * (d + 0.5) / ND) for d in range(ND)]
SIN = [math.sin(2.0 * math.pi * (d + 0.5) / ND) for d in range(ND)]


def rows_of(values):
    row = lax.broadcasted_iota(jnp.int32, (8, 128), 0)
    out = jnp.full((8, 128), values[0], jnp.float32)
    for s in range(1, 8):
        out = jnp.where(row == s, values[s], out)
    return out


def wide(v):
    return jnp.concatenate([v] * (NY // 128), axis=1)


def block_coeffs(first, quadrant):
    band = jnp.full((8, 128), first // ND, jnp.int32).astype(jnp.float32)
    speed = cfl_scale / (1.0 + 0.1 * band)
    c = rows_of([abs(COS[8 * quadrant + s]) for s in range(8)])
    n = rows_of([abs(SIN[8 * quadrant + s]) for s in range(8)])
    return wide(speed * c), wide(speed * n)


def substep(field, beside, ax, ay, sea, north):
    lane = lax.broadcasted_iota(jnp.int32, field.shape, 1)
    if north:
        up = jnp.where(lane == 0, 0.0, pltpu.roll(field, 1, 1))
    else:
        up = jnp.where(lane == NY - 1, 0.0, pltpu.roll(field, NY - 1, 1))
    return (field - ax * (field - beside) - ay * (field - up)) * sea


def code(v):
    return (v * Q + 0.5).astype(jnp.int32)


def decode(w):
    return w.astype(jnp.float32) * (1.0 / Q)


def low(w):
    return w & 0xFFFF


def high(w):
    return lax.shift_right_logical(w, 16)


def column(ref, row, col):
    return ref[pl.ds(row, 8), col * NY:(col + 1) * NY]


def sea_row(sea_ref, col):
    return jnp.broadcast_to(sea_ref[0:1, col * NY:(col + 1) * NY], (8, NY))


def edge_kernel(first_ref, last_ref, sea_ref, right_ref, left_ref):
    me = lax.axis_index("comp")
    sea_first = sea_row(sea_ref, 0).astype(jnp.float32)
    sea_last = sea_row(sea_ref, COLS - 1).astype(jnp.float32)

    def pair(i, carry):
        turn = (i + me) % 2
        for t in range(2):
            @pl.when(turn == t)
            def _():
                north = t == 0
                east_q, west_q = (0, 1) if north else (3, 2)
                east_row = pl.multiple_of(16 * i + 8 * t, 8)
                west_row = pl.multiple_of(16 * i + 8 * (1 - t), 8)
                at = pl.multiple_of(8 * i, 8)
                ax, ay = block_coeffs(me * 144 + east_row, east_q)
                f0 = last_ref[pl.ds(east_row, 8), NY:]
                f1 = substep(f0, last_ref[pl.ds(east_row, 8), :NY], ax, ay, sea_last, north)
                right_ref[pl.ds(at, 8), :] = code(f0) | (code(f1) << 16)
                ax, ay = block_coeffs(me * 144 + west_row, west_q)
                f0 = first_ref[pl.ds(west_row, 8), :NY]
                f1 = substep(f0, first_ref[pl.ds(west_row, 8), NY:], ax, ay, sea_first, north)
                left_ref[pl.ds(at, 8), :] = code(f0) | (code(f1) << 16)
        return carry

    lax.fori_loop(0, PAIRS, pair, 0)


def edges(spectrum, sea):
    count = spectrum.shape[0]
    shape = jax.ShapeDtypeStruct((PAIRS * 8, NY), jnp.int32)
    return pl.pallas_call(
        edge_kernel,
        grid=(1,),
        in_specs=[
            pl.BlockSpec((count, 2 * NY), lambda i: (0, 0)),
            pl.BlockSpec((count, 2 * NY), lambda i: (0, 3)),
            pl.BlockSpec((1, COLS * NY), lambda i: (0, 0)),
        ],
        out_specs=[pl.BlockSpec((PAIRS * 8, NY), lambda i: (0, 0))] * 2,
        out_shape=(shape, shape),
        name="edges",
    )(spectrum, spectrum, sea)


def move_kernel(first_pair, pairs, x_hbm, west_ref, east_ref, sea_ref, *rest):
    outs, (x_ref, sea8, low_words, words, stage, in_sems, out_sems) = rest[:8], rest[8:]
    me = lax.axis_index("comp")

    def load(i):
        rows = pl.ds(pl.multiple_of(16 * (first_pair + i), 16), 16)
        return pltpu.make_async_copy(x_hbm.at[rows, :], x_ref.at[i], in_sems.at[i])

    def store(i, k):
        rows = pl.ds(pl.multiple_of(i * 64, 64), 64)
        return pltpu.make_async_copy(stage.at[k, rows, :], outs[k].at[rows, :], out_sems.at[i, k])

    for i in range(pairs):
        load(i).start()
    for col in range(COLS):
        sea8[col] = sea_row(sea_ref, col).astype(jnp.float32)

    def block(i, half, quadrant, finish):
        p = first_pair + i
        north = quadrant in (0, 1)
        east = quadrant in (0, 3)
        ax, ay = block_coeffs(me * 144 + 16 * p + 8 * half, quadrant)
        edge = (west_ref if east else east_ref)[pl.ds(pl.multiple_of(8 * p, 8), 8), :]
        beside0, beside1 = decode(low(edge)), decode(high(edge))
        for col in (range(COLS) if east else range(COLS - 1, -1, -1)):
            f0 = x_ref[i, 8 * half:8 * half + 8, col * NY:(col + 1) * NY]
            sea = sea8[col]
            f1 = substep(f0, beside0, ax, ay, sea, north)
            f2 = substep(f1, beside1, ax, ay, sea, north)
            beside0, beside1 = f0, f1
            finish(col, code(f2))

    def pair(i, carry):
        load(i).wait()
        turn = (first_pair + i + me) % 2

        def keep(col, q):
            low_words[col] = q

        def join(col, q):
            w = low_words[col] | (q << 16)
            for k in range(8):
                words[pl.ds(col * 64 + k, 8, stride=8), :] = w[:, k * 128:(k + 1) * 128]

        for t in range(2):
            @pl.when(turn == t)
            def _():
                block(i, 0, 2 * t, keep)
                block(i, 1, 2 * t + 1, join)
        for k in range(8):
            col = (me + k) % 8
            stage[k, pl.ds(pl.multiple_of(i * 64, 64), 64), :] = words[pl.ds(pl.multiple_of(col * 64, 64), 64), :]
        for k in range(8):
            store(i, k).start()
        return carry

    lax.fori_loop(0, pairs, pair, 0)

    def drain(i, carry):
        for k in range(8):
            store(i, k).wait()
        return carry

    lax.fori_loop(0, pairs, drain, 0)


def moved(spectrum, west, east, sea, first_pair, pairs):
    whole = pl.BlockSpec(memory_space=pltpu.VMEM)
    shape = jax.ShapeDtypeStruct((pairs * 64, 128), jnp.int32)
    return pl.pallas_call(
        functools.partial(move_kernel, first_pair, pairs),
        in_specs=[pl.BlockSpec(memory_space=pl.ANY), whole, whole, whole],
        out_specs=[pl.BlockSpec(memory_space=pl.ANY)] * 8,
        out_shape=(shape,) * 8,
        scratch_shapes=[
            pltpu.VMEM((pairs, 16, COLS * NY), jnp.float32),
            pltpu.VMEM((COLS, 8, NY), jnp.float32),
            pltpu.VMEM((COLS, 8, NY), jnp.int32),
            pltpu.VMEM((COLS * 64, 128), jnp.int32),
            pltpu.VMEM((8, pairs * 64, 128), jnp.int32),
            pltpu.SemaphoreType.DMA((pairs,)),
            pltpu.SemaphoreType.DMA((pairs, 8)),
        ],
        name="move",
    )(spectrum, west, east, sea)


def finish_kernel(chunks, plus_ref, minus_ref, fid_ref, *rest):
    n = 8 * len(chunks)
    pieces = rest[:n]
    (wind_ref, route_ref, point_ref, point_t_ref, mine_ref, other_ref, out_ref,
     field, growth, scr, ohp, ohs, isf, buf, sems) = rest[n:]
    me = lax.axis_index("comp")

    total = jnp.zeros((8, 128), jnp.float32)
    for n_chunk, (first_pair, pairs) in enumerate(chunks):
        for k in range(8):
            src = (me - k) % 8
            ref = pieces[n_chunk * 8 + k]

            def unpack(i, sums, ref=ref, src=src, first_pair=first_pair):
                sums = list(sums)
                base = src * (144 * 8) + (first_pair + i) * 128
                for c in range(8):
                    w = ref[pl.ds(pl.multiple_of(i * 64 + c * 8, 8), 8), :]
                    a, b = decode(low(w)), decode(high(w))
                    field[pl.ds(pl.multiple_of(base + c * 8, 8), 8), :] = a
                    field[pl.ds(pl.multiple_of(base + 64 + c * 8, 8), 8), :] = b
                    sums[c % 4] = sums[c % 4] + (a + b)
                return tuple(sums)

            sums = lax.fori_loop(0, pairs, unpack, (jnp.zeros((8, 128), jnp.float32),) * 4)
            total = total + ((sums[0] + sums[1]) + (sums[2] + sums[3]))
    mean = total * (1.0 / NC)

    east_wind, north_wind = wind_ref[0:8, :], wind_ref[8:16, :]
    for d in range(ND):
        growth[d] = jnp.maximum(COS[d] * east_wind + SIN[d] * north_wind, 0.0)

    slot_of = jnp.broadcast_to(point_ref[0:1, :], (NY, 128))
    ohp[...] = (lax.broadcasted_iota(jnp.int32, (NY, 128), 0) == slot_of).astype(jnp.float32).astype(jnp.bfloat16)
    for k in range(8):
        lane = lax.broadcasted_iota(jnp.int32, (128, 128), 1) + k * 128
        hit = (lane == point_t_ref[...]).astype(jnp.float32)
        ohs[0:128, k * 128:(k + 1) * 128] = hit.astype(jnp.bfloat16)
        ohs[128:256, k * 128:(k + 1) * 128] = hit.astype(jnp.bfloat16)
        isf[:, k * 128:(k + 1) * 128] = jnp.broadcast_to(jnp.sum(hit, axis=0, keepdims=True), (8, 128))
    lane4 = lax.broadcasted_iota(jnp.int32, (32, 128), 1) // 32
    zero = jnp.zeros((32, 128), jnp.float32).astype(jnp.bfloat16)

    def group(g, carry):
        for j in range(4):
            f = g * 4 + j
            band = jnp.full((8, 128), f, jnp.int32).astype(jnp.float32)
            base = 1.0 - break_rate * mean * (0.5 + band * (1.0 / NF))
            gain = (band + 1.0) * (grow_rate / NF)
            for d in range(ND):
                c = f * ND + d
                here = field[pl.ds(pl.multiple_of(c * 8, 8), 8), :]
                a = field[pl.ds(pl.multiple_of(plus_ref[c] * 8, 8), 8), :]
                b = field[pl.ds(pl.multiple_of(minus_ref[c] * 8, 8), 8), :]
                value = here * (base + gain * growth[d] + (pair_rate * here) * (a + b) - (2.0 * pair_rate) * (a * b))
                local = j * ND + d
                scr[pl.ds((local // 8) * 64 + local % 8, 8, stride=8), :] = value

        cells = jnp.zeros((128, 128), jnp.float32)
        for k in range(8):
            xk = jnp.concatenate([scr[cb * 64 + k * 8:cb * 64 + k * 8 + 8, :] for cb in range(16)], axis=0)
            cells = cells + jnp.dot(xk.astype(jnp.bfloat16), ohp[k * 128:(k + 1) * 128, :],
                                    preferred_element_type=jnp.float32)
        cells = cells.astype(jnp.bfloat16)
        route = jnp.broadcast_to(route_ref[0:1, :], (128, 128))
        none = jnp.zeros((128, 128), jnp.float32).astype(jnp.bfloat16)

        def table(ref, t):
            m = ref[pl.ds(pl.multiple_of(t * 288 + g * 32, 32), 32), :]
            return jnp.concatenate([jnp.where(lane4 == j, m, zero) for j in range(4)], axis=0)

        farmed = jnp.zeros((128, 128), jnp.float32)
        for t in range(16):
            left = jnp.concatenate([table(mine_ref, t), table(other_ref, t)], axis=1)
            right = jnp.concatenate([jnp.where(route == fid_ref[t], cells, none),
                                     jnp.where(route == fid_ref[16 + t], cells, none)], axis=0)
            farmed = farmed + jnp.dot(left, right, preferred_element_type=jnp.float32)
        top = farmed.astype(jnp.bfloat16)
        rest_of = (farmed - top.astype(jnp.float32)).astype(jnp.bfloat16)
        both = jnp.concatenate([top, rest_of], axis=1)
        for k in range(8):
            spread = jnp.dot(both, ohs[:, k * 128:(k + 1) * 128], preferred_element_type=jnp.float32)
            on = isf[:, k * 128:(k + 1) * 128] > 0.5
            for cb in range(16):
                v = jnp.where(on, spread[cb * 8:cb * 8 + 8, :], scr[cb * 64 + k * 8:cb * 64 + k * 8 + 8, :])
                buf[g, cb * 8:cb * 8 + 8, k * 128:(k + 1) * 128] = v
        store(g).start()
        return carry

    def store(g):
        return pltpu.make_async_copy(buf.at[g], out_ref.at[pl.ds(pl.multiple_of(g * 128, 128), 128), :], sems.at[g])

    lax.fori_loop(0, GROUPS_F, group, 0)

    def drain(g, carry):
        store(g).wait()
        return carry

    lax.fori_loop(0, GROUPS_F, drain, 0)


def finished(chunks, pieces, plus, minus, fid, wind, route, point, point_t, mine, other):
    whole = pl.BlockSpec(memory_space=pltpu.VMEM)
    smem = pl.BlockSpec(memory_space=pltpu.SMEM)
    return pl.pallas_call(
        functools.partial(finish_kernel, chunks),
        in_specs=[smem] * 3 + [whole] * (len(pieces) + 6),
        out_specs=pl.BlockSpec(memory_space=pl.ANY),
        out_shape=jax.ShapeDtypeStruct((NC, NY), jnp.float32),
        scratch_shapes=[
            pltpu.VMEM((NC * 8, 128), jnp.float32),
            pltpu.VMEM((ND, 8, 128), jnp.float32),
            pltpu.VMEM((1024, 128), jnp.float32),
            pltpu.VMEM((NY, 128), jnp.bfloat16),
            pltpu.VMEM((256, NY), jnp.bfloat16),
            pltpu.VMEM((8, NY), jnp.float32),
            pltpu.VMEM((GROUPS_F, 128, NY), jnp.float32),
            pltpu.SemaphoreType.DMA((GROUPS_F,)),
        ],
        name="finish",
    )(plus, minus, fid, *pieces, wind, route, point, point_t, mine, other)


def after(value, *others):
    return lax.optimization_barrier((value,) + others)[0]


def local(spectrum, sea_mask, wind_speed, wind_dir, dia_plus, dia_minus, farm_point, farm_route, farm_matrix):
    tiles, comps = lax.axis_size("tile"), lax.axis_size("comp")
    tile = lax.axis_index("tile")
    sea = sea_mask.reshape(1, -1)
    up = [(i, i + 1) for i in range(tiles - 1)]
    down = [(i + 1, i) for i in range(tiles - 1)]
    right, left = edges(spectrum, sea)
    west = lax.ppermute(right, "tile", up)
    east = lax.ppermute(left, "tile", down)

    chunks = ((0, PAIRS),)
    pieces = []
    for first, pairs in chunks:
        out = moved(spectrum, west, east, sea, first, pairs)
        pieces.append(out[0])
        for k in range(1, comps):
            pieces.append(lax.ppermute(out[k], "comp", [(i, (i + k) % comps) for i in range(comps)]))

    def shift(dx, dy, dc):
        return [(x * 8 + y * 2 + c, ((x + dx) % 4) * 8 + ((y + dy) % 4) * 2 + (c ^ dc))
                for x in range(4) for y in range(4) for c in range(2)]

    table = after(farm_matrix, right)[0]
    table = table.reshape(GROUPS_F, 4, ND, ND).transpose(0, 2, 1, 3).reshape(GROUPS_F * ND, 128)
    by_x = jnp.concatenate([table] + [lax.ppermute(table, "tile", shift(k, 0, 0)) for k in (1, 2, 3)], axis=0)
    by_x = after(by_x, out[1])
    mine = jnp.concatenate([by_x] + [lax.ppermute(by_x, "tile", shift(0, k, 0)) for k in (1, 2, 3)], axis=0)
    other = lax.ppermute(mine, "tile", shift(0, 0, 1))
    x, y, core = tile // 8, (tile // 2) % 4, tile % 2
    order = jnp.arange(16, dtype=jnp.int32)
    fid = ((x - order % 4) % 4) * 8 + ((y - order // 4) % 4) * 2
    fid = jnp.concatenate([fid + core, fid + (1 - core)]).astype(jnp.int32)

    speed, direction = after((wind_speed, wind_dir), out[1])
    wind = jnp.stack([speed * jnp.cos(direction), speed * jnp.sin(direction)]).reshape(16, 128)
    point = jnp.pad(farm_point.reshape(SLOTS), (0, 128 - SLOTS), constant_values=-1)
    route = jnp.pad(farm_route.reshape(SLOTS), (0, 128 - SLOTS), constant_values=-1)
    point_t = jnp.broadcast_to(point[:, None], (128, 128))
    return finished(chunks, pieces, dia_plus, dia_minus, fid, wind, route.reshape(1, 128), point.reshape(1, 128),
                    point_t, mine, other)


def solution(mesh):
    return jax.shard_map(
        local,
        mesh=mesh,
        in_specs=(
            P("comp", "tile"),
            P("tile"),
            P(("tile", "comp")),
            P(("tile", "comp")),
            P(),
            P(),
            P("tile", "comp", None),
            P("tile", "comp", None, None),
            P("tile", None, None, None),
        ),
        out_specs=P(None, ("tile", "comp")),
        check_vma=False,
    )
```

```python
import functools
import math

import jax
import jax.numpy as jnp
from jax import lax
from jax.experimental import pallas as pl
from jax.experimental.pallas import tpu as pltpu
from jax.sharding import PartitionSpec as P


NF = 36
ND = 32
NC = 1152
NY = 1024
COLS = 8
PAIRS = 9
SLOTS = 64
GROUPS_F = 9
FARMS = 32
Q = 65535.0

cfl_scale = 0.6
grow_rate = 0.35
break_rate = 0.6
pair_rate = 0.5


COS = [math.cos(2.0 * math.pi * (d + 0.5) / ND) for d in range(ND)]
SIN = [math.sin(2.0 * math.pi * (d + 0.5) / ND) for d in range(ND)]


def rows_of(values):
    row = lax.broadcasted_iota(jnp.int32, (8, 128), 0)
    out = jnp.full((8, 128), values[0], jnp.float32)
    for s in range(1, 8):
        out = jnp.where(row == s, values[s], out)
    return out


def wide(v, tiles):
    return jnp.concatenate([v] * tiles, axis=1)


def block_coeffs(first, quadrant, tiles=NY // 128):
    band = jnp.full((8, 128), first // ND, jnp.int32).astype(jnp.float32)
    speed = cfl_scale / (1.0 + 0.1 * band)
    c = rows_of([abs(COS[8 * quadrant + s]) for s in range(8)])
    n = rows_of([abs(SIN[8 * quadrant + s]) for s in range(8)])
    return wide(speed * c, tiles), wide(speed * n, tiles)


def substep(field, beside, ax, ay, sea, north):
    lane = lax.broadcasted_iota(jnp.int32, field.shape, 1)
    if north:
        up = jnp.where(lane == 0, 0.0, pltpu.roll(field, 1, 1))
    else:
        up = jnp.where(lane == NY - 1, 0.0, pltpu.roll(field, NY - 1, 1))
    return (field - ax * (field - beside) - ay * (field - up)) * sea


def code(v):
    return (v * Q + 0.5).astype(jnp.int32)


def decode(w):
    return w.astype(jnp.float32) * (1.0 / Q)


def low(w):
    return w & 0xFFFF


def high(w):
    return lax.shift_right_logical(w, 16)


def sea_row(sea_ref, col):
    return jnp.broadcast_to(sea_ref[0:1, col * NY:(col + 1) * NY], (8, NY))


def edge_kernel(x_hbm, sea_hbm, right_ref, left_ref, last_ref, first_ref, sea_ref, sems, sea_sem):
    me = lax.axis_index("comp")
    sea_load = pltpu.make_async_copy(sea_hbm, sea_ref, sea_sem)
    sea_load.start()

    def loads(i):
        t = (i + me) % 2
        east_row = pl.multiple_of(16 * i + 8 * t, 8)
        west_row = pl.multiple_of(16 * i + 8 * (1 - t), 8)
        return (
            pltpu.make_async_copy(x_hbm.at[pl.ds(east_row, 8), pl.ds((COLS - 2) * NY, 2 * NY)], last_ref.at[i], sems.at[0, i]),
            pltpu.make_async_copy(x_hbm.at[pl.ds(west_row, 8), pl.ds(0, 2 * NY)], first_ref.at[i], sems.at[1, i]),
        )

    for i in range(PAIRS):
        for copy in loads(i):
            copy.start()
    sea_load.wait()
    sea_first = sea_row(sea_ref, 0).astype(jnp.float32)
    sea_last = sea_row(sea_ref, COLS - 1).astype(jnp.float32)

    def pair(i, carry):
        turn = (i + me) % 2
        for copy in loads(i):
            copy.wait()
        at = pl.ds(pl.multiple_of(8 * i, 8), 8)
        for t in range(2):
            @pl.when(turn == t)
            def _():
                north = t == 0
                east_q, west_q = (0, 1) if north else (3, 2)
                ax, ay = block_coeffs(me * 144 + 16 * i + 8 * t, east_q)
                f0 = last_ref[i, :, NY:]
                f1 = substep(f0, last_ref[i, :, :NY], ax, ay, sea_last, north)
                right_ref[at, :] = code(f0) | (code(f1) << 16)
                ax, ay = block_coeffs(me * 144 + 16 * i + 8 * (1 - t), west_q)
                f0 = first_ref[i, :, :NY]
                f1 = substep(f0, first_ref[i, :, NY:], ax, ay, sea_first, north)
                left_ref[at, :] = code(f0) | (code(f1) << 16)
        return carry

    lax.fori_loop(0, PAIRS, pair, 0)


def edges(spectrum, sea):
    shape = jax.ShapeDtypeStruct((PAIRS * 8, NY), jnp.int32)
    whole = pl.BlockSpec(memory_space=pltpu.VMEM)
    return pl.pallas_call(
        edge_kernel,
        in_specs=[pl.BlockSpec(memory_space=pl.ANY)] * 2,
        out_specs=[whole] * 2,
        out_shape=(shape, shape),
        scratch_shapes=[
            pltpu.VMEM((PAIRS, 8, 2 * NY), jnp.float32),
            pltpu.VMEM((PAIRS, 8, 2 * NY), jnp.float32),
            pltpu.VMEM((1, COLS * NY), jnp.int32),
            pltpu.SemaphoreType.DMA((2, PAIRS)),
            pltpu.SemaphoreType.DMA,
        ],
        compiler_params=pltpu.CompilerParams(vmem_limit_bytes=59600 << 10),
        name="edges",
    )(spectrum, sea)


AHEAD = 3


def move_kernel(half, together, x_hbm, west_hbm, east_hbm, sea_hbm, *rest):
    n_out = 1 if together else 8
    outs = rest[:n_out]
    x_ref, west_ref, east_ref, sea_ref, sea8, sea8q, low_words, words, in_sems, side_sems = rest[n_out:]
    me = lax.axis_index("comp")
    start = half * (NY // 2)
    sides = [pltpu.make_async_copy(src, dst, side_sems.at[n]) for n, (src, dst) in enumerate(
        ((sea_hbm, sea_ref), (west_hbm, west_ref), (east_hbm, east_ref)))]

    def load(i):
        rows = pl.ds(pl.multiple_of(16 * i, 16), 16)
        return pltpu.make_async_copy(x_hbm.at[rows, :], x_ref.at[i], in_sems.at[i])

    sides[0].start()
    load(0).start()
    for side in sides[1:]:
        side.start()
    for i in range(1, AHEAD):
        load(i).start()
    sides[0].wait()
    for col in range(COLS):
        sea = sea_row(sea_ref, col).astype(jnp.float32)
        sea8[col] = sea
        sea8q[col] = sea * Q
    for side in sides[1:]:
        side.wait()

    def block(i, half_of, quadrant, finish):
        north = quadrant in (0, 1)
        east = quadrant in (0, 3)
        begin = start - 128 if north and half == 1 else start
        width = NY // 2 if north == (half == 0) else NY // 2 + 128
        ax, ay = block_coeffs(me * 144 + 16 * i + 8 * half_of, quadrant, width // 128)
        keep_of = 1.0 - ax - ay
        edge = (west_ref if east else east_ref)[pl.ds(pl.multiple_of(8 * i, 8), 8), begin:begin + width]
        beside0, beside1 = decode(low(edge)), decode(high(edge))
        first = 128 if begin < start else 0

        def step(field, beside, sea):
            lane = lax.broadcasted_iota(jnp.int32, (8, 128), 1)
            if north:
                up = pltpu.roll(field, 1, 1)
                if half == 0:
                    up = jnp.concatenate([jnp.where(lane == 0, 0.0, up[:, :128]), up[:, 128:]], axis=1)
            else:
                up = pltpu.roll(field, width - 1, 1)
                if half == 1:
                    up = jnp.concatenate([up[:, :-128], jnp.where(lane == 127, 0.0, up[:, -128:])], axis=1)
            return (keep_of * field + ax * beside + ay * up) * sea

        for col in (range(COLS) if east else range(COLS - 1, -1, -1)):
            f0 = x_ref[i, 8 * half_of:8 * half_of + 8, col * NY + begin:col * NY + begin + width]
            f1 = step(f0, beside0, sea8[col, :, begin:begin + width])
            f2 = step(f1, beside1, sea8q[col, :, begin:begin + width])
            beside0, beside1 = f0, f1
            finish(col, (f2[:, first:first + NY // 2] + 0.5).astype(jnp.int32))

    def pair(i, carry):
        load(i).wait()

        @pl.when(i + AHEAD < PAIRS)
        def _():
            load(i + AHEAD).start()

        turn = (i + me) % 2

        def keep(col, q):
            low_words[col] = q

        def join(col, q):
            w = low_words[col] | (q << 16)
            for k in range(4):
                words[pl.ds(col * 32 + k, 8, stride=4), :] = w[:, k * 128:(k + 1) * 128]

        for t in range(2):
            @pl.when(turn == t)
            def _():
                block(i, 0, 2 * t, keep)
                block(i, 1, 2 * t + 1, join)
        rows = pl.ds(pl.multiple_of(i * 32, 32), 32)
        for k in range(8):
            col = k if together else (me + k) % 8
            value = words[pl.ds(pl.multiple_of(col * 32, 32), 32), :]
            if together:
                outs[0][k, rows, :] = value
            else:
                outs[k][rows, :] = value
        return carry

    lax.fori_loop(0, PAIRS, pair, 0)


def moved(spectrum, west, east, sea, half, together):
    whole = pl.BlockSpec(memory_space=pltpu.VMEM)
    anywhere = pl.BlockSpec(memory_space=pl.ANY)
    rows = PAIRS * 32
    if together:
        out_shape, out_specs = jax.ShapeDtypeStruct((8, rows, 128), jnp.int32), whole
    else:
        out_shape, out_specs = (jax.ShapeDtypeStruct((rows, 128), jnp.int32),) * 8, [whole] * 8
    return pl.pallas_call(
        functools.partial(move_kernel, half, together),
        in_specs=[anywhere] * 4,
        out_specs=out_specs,
        out_shape=out_shape,
        scratch_shapes=[
            pltpu.VMEM((PAIRS, 16, COLS * NY), jnp.float32),
            pltpu.VMEM((PAIRS * 8, NY), jnp.int32),
            pltpu.VMEM((PAIRS * 8, NY), jnp.int32),
            pltpu.VMEM((1, COLS * NY), jnp.int32),
            pltpu.VMEM((COLS, 8, NY), jnp.float32),
            pltpu.VMEM((COLS, 8, NY), jnp.float32),
            pltpu.VMEM((COLS, 8, NY // 2), jnp.int32),
            pltpu.VMEM((COLS * 32, 128), jnp.int32),
            pltpu.SemaphoreType.DMA((PAIRS,)),
            pltpu.SemaphoreType.DMA((3,)),
        ],
        compiler_params=pltpu.CompilerParams(vmem_limit_bytes=59600 << 10),
        name="move",
    )(spectrum, west, east, sea)


def pair_kernel(a_ref, b_ref, c_ref, d_ref, out_ref):
    for n, (one, two) in enumerate(((a_ref, b_ref), (c_ref, d_ref))):
        for g in range(GROUPS_F):
            a, b = one[g * 32:g * 32 + 32, :], two[g * 32:g * 32 + 32, :]
            at = (n * GROUPS_F + g) * 64
            out_ref[at:at + 32, :] = jnp.concatenate([a[:, :64], b[:, :64]], axis=1)
            out_ref[at + 32:at + 64, :] = jnp.concatenate([a[:, 64:], b[:, 64:]], axis=1)


def paired(tables):
    whole = pl.BlockSpec(memory_space=pltpu.VMEM)
    return pl.pallas_call(
        pair_kernel,
        in_specs=[whole] * 4,
        out_specs=whole,
        out_shape=jax.ShapeDtypeStruct((4 * GROUPS_F * 32, 128), jnp.bfloat16),
        compiler_params=pltpu.CompilerParams(vmem_limit_bytes=4 << 20),
        name="pair",
    )(*tables)


FRONT = 8
MARKS = ((1536, 128), jnp.bfloat16)
VALUES = ((160, 128), jnp.float32)


def prepare(half, speed_ref, direction_ref, point_ref, route_ref, marks, values):
    tile = lax.axis_index("tile")
    start = half * (NY // 2)
    x, y, core = tile // 8, (tile // 2) % 4, tile % 2
    route = route_ref[0:1, :]
    route = jnp.broadcast_to(jnp.concatenate([route, route], axis=1), (16, 128))
    for n in range(FARMS):
        farm = ((x - n % 4 + 4) % 4) * 8 + ((y - (n // 4) % 4 + 4) % 4) * 2 + (core + n // 16) % 2
        marks[1024 + 16 * n:1040 + 16 * n, :] = (route == farm).astype(jnp.float32).astype(jnp.bfloat16)
    point = point_ref[0:1, :]
    slot_of = jnp.broadcast_to(jnp.concatenate([point, point], axis=1), (128, 128)) - start
    point_t = jnp.transpose(slot_of)
    for k in range(4):
        hit = lax.broadcasted_iota(jnp.int32, (128, 128), 0) + k * 128 == slot_of
        marks[128 * k:128 * k + 128, :] = hit.astype(jnp.float32).astype(jnp.bfloat16)
        hit = (lax.broadcasted_iota(jnp.int32, (128, 128), 1) + k * 128 == point_t).astype(jnp.float32)
        marks[512 + 128 * k:640 + 128 * k, :] = hit.astype(jnp.bfloat16)
        values[128 + 8 * k:136 + 8 * k, :] = jnp.broadcast_to(jnp.sum(hit, axis=0, keepdims=True), (8, 128))
    speed, direction = speed_ref[4 * half:4 * half + 4, :], direction_ref[4 * half:4 * half + 4, :]
    speed = jnp.concatenate([speed, speed], axis=0)
    direction = jnp.concatenate([direction, direction], axis=0)
    east_wind, north_wind = speed * jnp.cos(direction), speed * jnp.sin(direction)
    upper = lax.broadcasted_iota(jnp.int32, (8, 128), 0) < 4
    for n in range(ND // 2):
        cos = jnp.where(upper, COS[2 * n], COS[2 * n + 1])
        sin = jnp.where(upper, SIN[2 * n], SIN[2 * n + 1])
        values[8 * n:8 * n + 8, :] = jnp.maximum(cos * east_wind + sin * north_wind, 0.0)


def finish_kernel(half, together, plus_ref, minus_ref, *rest):
    n = 1 if together else 8
    pieces = rest[:n]
    tables = rest[n:n + 2]
    if half == 0:
        speed_ref, direction_ref, point_ref, route_ref = rest[n + 2:n + 6]
    rest = rest[n + 6:] if half == 0 else rest[n + 2:]
    if half == 0:
        out_ref, later_marks, later_values, field, scr_a, scr_b, buf, marks, values, sem = rest
        prepare(0, speed_ref, direction_ref, point_ref, route_ref, marks, values)
        prepare(1, speed_ref, direction_ref, point_ref, route_ref, later_marks, later_values)
    else:
        marks, values, _, out_ref, field, scr_a, scr_b, buf, sem = rest
    me = lax.axis_index("comp")
    start = half * (NY // 2)
    left_lanes = lax.broadcasted_iota(jnp.int32, (32, 128), 1) < 64
    upper = lax.broadcasted_iota(jnp.int32, (8, 128), 0) < 4

    def unpack(i, sums):
        sums = list(sums)
        for k in range(8):
            src = k if together else (me - k + 8) % 8
            base = FRONT + src * (144 * 4) + i * 64
            for v in range(4):
                rows = pl.ds(pl.multiple_of(i * 32 + v * 8, 8), 8)
                w = pieces[0][k, rows, :] if together else pieces[k][rows, :]
                a, b = decode(low(w)), decode(high(w))
                field[pl.ds(pl.multiple_of(base + v * 8, 8), 8), :] = a
                field[pl.ds(pl.multiple_of(base + 32 + v * 8, 8), 8), :] = b
                sums[v] = sums[v] + (a + b)
        return tuple(sums)

    sums = lax.fori_loop(0, PAIRS, unpack, (jnp.zeros((8, 128), jnp.float32),) * 4)
    total = (sums[0] + sums[1]) + (sums[2] + sums[3])
    mean = (total + pltpu.roll(total, 4, 0)) * (break_rate / NC)

    def partner(ref, c):
        return jnp.where(upper, field[pl.ds(ref[c], 8), :], field[pl.ds(ref[c + 1], 8), :])

    def source(g, scr):
        for j in range(4):
            f = g * 4 + j
            band = jnp.full((8, 128), f, jnp.int32).astype(jnp.float32)
            base = 1.0 - mean * (0.5 + band * (1.0 / NF))
            gain = (band + 1.0) * (grow_rate / NF)
            for d in range(0, ND, 2):
                c = f * ND + d
                here = field[pl.ds(pl.multiple_of(FRONT + c * 4, 8), 8), :]
                a, b = partner(plus_ref, c), partner(minus_ref, c)
                value = here * (base + gain * values[d * 4:d * 4 + 8, :]
                                + (pair_rate * here) * (a + b) - (2.0 * pair_rate) * (a * b))
                local = j * ND + d
                scr[local * 4:local * 4 + 8, :] = value

    def farm(g, scr):
        def cut(cb, k):
            return scr[pl.ds(cb * 32 + k, 8, stride=4), :]

        cells = jnp.zeros((128, 128), jnp.float32)
        for k in range(0, 4, 2):
            xk = [jnp.concatenate([cut(cb, kk) for cb in range(16)], axis=0).astype(jnp.bfloat16) for kk in (k, k + 1)]
            cells = cells + jnp.dot(jnp.concatenate(xk, axis=1), marks[k * 128:(k + 2) * 128, :],
                                    preferred_element_type=jnp.float32)
        both = []
        for p in range(2):
            rows = [cells[64 * p:64 * p + 32, :], cells[64 * p + 32:64 * p + 64, :]]
            own = jnp.concatenate([jnp.where(left_lanes, rows[0], 0.0), jnp.where(left_lanes, 0.0, rows[1])], axis=0)
            own = own.astype(jnp.bfloat16)
            farmed = jnp.zeros((32, 128), jnp.float32)
            for n in range(8):
                left = [tables[m // 8][pl.ds(pl.multiple_of((m % 8 * GROUPS_F + g) * 64 + 32 * p, 32), 32), :]
                        for m in (2 * n, 2 * n + 1)]
                right = [own * jnp.concatenate([marks[1024 + 16 * m:1040 + 16 * m, :]] * 4, axis=0)
                         for m in range(4 * n, 4 * n + 4)]
                farmed = farmed + jnp.dot(jnp.concatenate(left, axis=1), jnp.concatenate(right, axis=0),
                                          preferred_element_type=jnp.float32)
            top = farmed.astype(jnp.bfloat16).astype(jnp.float32)
            rest_of = farmed - top
            both.append(jnp.where(left_lanes, top, pltpu.roll(rest_of, 64, 1)).astype(jnp.bfloat16))
            both.append(jnp.where(left_lanes, pltpu.roll(top, 64, 1), rest_of).astype(jnp.bfloat16))
        both = jnp.concatenate(both, axis=0)
        for k in range(0, 4, 2):
            slots = jnp.concatenate([marks[512 + 128 * kk:640 + 128 * kk, :] for kk in (k, k + 1)], axis=1)
            spread = jnp.dot(both, slots, preferred_element_type=jnp.float32)
            for kk in range(2):
                at = slice((k + kk) * 128, (k + kk + 1) * 128)
                on = values[128 + 8 * (k + kk):136 + 8 * (k + kk), :] > 0.5
                for cb in range(16):
                    row = pl.ds(pl.multiple_of(g * 128 + cb * 8, 8), 8)
                    buf[row, at] = jnp.where(on, spread[cb * 8:cb * 8 + 8, kk * 128:(kk + 1) * 128], cut(cb, k + kk))

    here_points = pl.ds(start, NY // 2)

    def store(g):
        rows = pl.ds(pl.multiple_of(g * 128, 128), 128)
        pltpu.make_async_copy(buf.at[rows, :], out_ref.at[rows, here_points], sem).start()

    source(0, scr_a)
    for g in range(GROUPS_F - 1):
        here, there = (scr_a, scr_b) if g % 2 == 0 else (scr_b, scr_a)
        source(g + 1, there)
        farm(g, here)
        store(g)
    farm(GROUPS_F - 1, scr_a)
    store(GROUPS_F - 1)
    pltpu.make_async_copy(buf, out_ref.at[:, here_points], sem).wait()


def finished(half, together, pieces, tables, facts, plus, minus, out=None):
    whole = pl.BlockSpec(memory_space=pltpu.VMEM)
    smem = pl.BlockSpec(memory_space=pltpu.SMEM)
    anywhere = pl.BlockSpec(memory_space=pl.ANY)
    operands = [plus, minus, *pieces, *tables, *facts]
    in_specs = [smem] * 2 + [whole] * (len(pieces) + len(tables) + len(facts))
    out_specs, out_shape = [anywhere], [jax.ShapeDtypeStruct((NC, NY), jnp.float32)]
    ready = [pltpu.VMEM(*MARKS), pltpu.VMEM(*VALUES)]
    aliases = {}
    if half == 0:
        out_specs += [whole] * 2
        out_shape += [jax.ShapeDtypeStruct(*MARKS), jax.ShapeDtypeStruct(*VALUES)]
    else:
        aliases = {len(operands): 0}
        operands.append(out)
        in_specs.append(anywhere)
        ready = []
    return pl.pallas_call(
        functools.partial(finish_kernel, half, together),
        in_specs=in_specs,
        out_specs=out_specs,
        out_shape=out_shape,
        input_output_aliases=aliases,
        scratch_shapes=[
            pltpu.VMEM((FRONT + NC * 4 + 8, 128), jnp.float32),
            pltpu.VMEM((512, 128), jnp.float32),
            pltpu.VMEM((512, 128), jnp.float32),
            pltpu.VMEM((NC, NY // 2), jnp.float32),
            *ready,
            pltpu.SemaphoreType.DMA,
        ],
        compiler_params=pltpu.CompilerParams(vmem_limit_bytes=20 << 20),
        name="finish",
    )(*operands)


def after(value, *others):
    return lax.optimization_barrier((value,) + others)[0]


def local(spectrum, sea_mask, wind_speed, wind_dir, dia_plus, dia_minus, farm_point, farm_route, farm_matrix):
    tiles, comps = lax.axis_size("tile"), lax.axis_size("comp")
    sea = sea_mask.reshape(1, -1)
    up = [(i, i + 1) for i in range(tiles - 1)]
    down = [(i + 1, i) for i in range(tiles - 1)]
    right, left = edges(spectrum, sea)
    west = lax.ppermute(right, "tile", up)
    east = lax.ppermute(left, "tile", down)

    ring = [[(i, (i + k) % comps) for i in range(comps)] for k in range(comps)]
    out = moved(spectrum, west, east, sea, 0, False)
    pieces = [out[0]]
    for k in range(1, comps):
        pieces.append(lax.ppermute(out[k], "comp", ring[k]))

    def shift(dx, dy, dc):
        return [(x * 8 + y * 2 + c, ((x + dx) % 4) * 8 + ((y + dy) % 4) * 2 + (c ^ dc))
                for x in range(4) for y in range(4) for c in range(2)]

    def spread(value, axis):
        parts = [value]
        for k in (1, 2, 3):
            parts.append(lax.ppermute(value, "tile", shift(k, 0, 0) if axis == "x" else shift(0, k, 0)))
        return parts

    table = after(farm_matrix, right)[0]
    table = table.reshape(GROUPS_F, 4, ND, ND).transpose(0, 2, 1, 3).reshape(GROUPS_F * ND, 128)
    mine = jnp.concatenate(spread(paired(spread(table, "x")), "y"), axis=0)
    other = lax.ppermute(mine, "tile", shift(0, 0, 1))

    second = moved(after(spectrum, out[1]), west, east, sea, 1, True)
    second = lax.all_to_all(second, "comp", split_axis=0, concat_axis=0, tiled=True)

    odd = 4 * (jnp.arange(NC, dtype=jnp.int32) % 2)
    plus, minus = after((dia_plus, dia_minus), out[1])
    plus, minus = FRONT + 4 * plus - odd, FRONT + 4 * minus - odd
    facts = (wind_speed.reshape(8, 128), wind_dir.reshape(8, 128), farm_point.reshape(1, SLOTS),
             farm_route.reshape(1, SLOTS))
    result, *ready = finished(0, False, pieces, (mine, other), facts, plus, minus)
    return finished(1, True, [second], (mine, other), ready, plus, minus, result)[0]


def solution(mesh):
    return jax.shard_map(
        local,
        mesh=mesh,
        in_specs=(
            P("comp", "tile"),
            P("tile"),
            P(("tile", "comp")),
            P(("tile", "comp")),
            P(),
            P(),
            P("tile", "comp", None),
            P("tile", "comp", None, None),
            P("tile", None, None, None),
        ),
        out_specs=P(None, ("tile", "comp")),
        check_vma=False,
    )
```

```python
import functools
import math

import jax
import jax.numpy as jnp
from jax import lax
from jax.experimental import pallas as pl
from jax.experimental.pallas import tpu as pltpu
from jax.sharding import PartitionSpec as P


NF = 36
ND = 32
NC = 1152
NY = 1024
COLS = 8
PAIRS = 9
SLOTS = 64
GROUPS_F = 9
FARMS = 32
Q = 65535.0

cfl_scale = 0.6
grow_rate = 0.35
break_rate = 0.6
pair_rate = 0.5


COS = [math.cos(2.0 * math.pi * (d + 0.5) / ND) for d in range(ND)]
SIN = [math.sin(2.0 * math.pi * (d + 0.5) / ND) for d in range(ND)]


def rows_of(values):
    row = lax.broadcasted_iota(jnp.int32, (8, 128), 0)
    out = jnp.full((8, 128), values[0], jnp.float32)
    for s in range(1, 8):
        out = jnp.where(row == s, values[s], out)
    return out


def wide(v, tiles):
    return jnp.concatenate([v] * tiles, axis=1)


def block_coeffs(first, quadrant, tiles=NY // 128):
    band = jnp.full((8, 128), first // ND, jnp.int32).astype(jnp.float32)
    speed = cfl_scale / (1.0 + 0.1 * band)
    c = rows_of([abs(COS[8 * quadrant + s]) for s in range(8)])
    n = rows_of([abs(SIN[8 * quadrant + s]) for s in range(8)])
    return wide(speed * c, tiles), wide(speed * n, tiles)


def code(v):
    return (v * Q + 0.5).astype(jnp.int32)


def decode(w):
    return w.astype(jnp.float32) * (1.0 / Q)


def low(w):
    return w & 0xFFFF


def high(w):
    return lax.shift_right_logical(w, 16)


def sea_row(sea_ref, col):
    return jnp.broadcast_to(sea_ref[0:1, col * NY:(col + 1) * NY], (8, NY))


AHEAD = 3
HALF = NY // 2


def move_kernel(late, *refs):
    if late:
        x_hbm, sea_hbm, west_ref, east_ref, out_ref = refs[:5]
    else:
        x_hbm, sea_hbm, *outs, right_ref, left_ref = refs[:12]
    x_ref, sea_ref, sea8, sea8q, words, in_sems, sea_sem = refs[-7:]
    me = lax.axis_index("comp")

    def load(i):
        rows = pl.ds(pl.multiple_of(16 * i, 16), 16)
        return pltpu.make_async_copy(x_hbm.at[rows, :], x_ref.at[i], in_sems.at[i])

    sea_load = pltpu.make_async_copy(sea_hbm, sea_ref, sea_sem)
    sea_load.start()
    for i in range(AHEAD):
        load(i).start()
    sea_load.wait()
    for col in range(COLS):
        sea = sea_row(sea_ref, col).astype(jnp.float32)
        sea8[col] = sea
        sea8q[col] = sea * Q

    def emit(col, f2):
        q = (f2 + 0.5).astype(jnp.int32)
        w = q[:, :HALF] | (q[:, HALF:] << 16)
        for k in range(4):
            words[pl.ds(col * 32 + k, 8, stride=4), :] = w[:, k * 128:(k + 1) * 128]

    def block(i, half_of, quadrant):
        north = quadrant in (0, 1)
        east = quadrant in (0, 3)
        ax, ay = block_coeffs(me * 144 + 16 * i + 8 * half_of, quadrant)
        keep_of = 1.0 - ax - ay
        at = pl.ds(pl.multiple_of(8 * i, 8), 8)

        def field(col):
            return x_ref[i, 8 * half_of:8 * half_of + 8, col * NY:(col + 1) * NY]

        def step(value, beside, sea):
            lane = lax.broadcasted_iota(jnp.int32, (8, 128), 1)
            if north:
                up = pltpu.roll(value, 1, 1)
                up = jnp.concatenate([jnp.where(lane == 0, 0.0, up[:, :128]), up[:, 128:]], axis=1)
            else:
                up = pltpu.roll(value, NY - 1, 1)
                up = jnp.concatenate([up[:, :-128], jnp.where(lane == 127, 0.0, up[:, -128:])], axis=1)
            return (keep_of * value + ax * beside + ay * up) * sea

        if late:
            edge = (west_ref if east else east_ref)[at, :]
            beside0, beside1 = decode(low(edge)), decode(high(edge))
            for col in ((0, 1) if east else (7, 6, 5, 4, 3, 2)):
                f0 = field(col)
                f1 = step(f0, beside0, sea8[col])
                emit(col, step(f1, beside1, sea8q[col]))
                beside0, beside1 = f0, f1
            return
        cols = (0, 1, 2, 3, 4, 5, 6, 7) if east else (3, 2, 1, 0)
        beside0, beside1 = field(cols[0]), None
        for col in cols[1:]:
            f0 = field(col)
            f1 = step(f0, beside0, sea8[col])
            if beside1 is not None:
                emit(col, step(f1, beside1, sea8q[col]))
            beside0, beside1 = f0, f1
        (right_ref if east else left_ref)[at, :] = code(beside0) | (code(beside1) << 16)

    def pair(i, carry):
        load(i).wait()

        @pl.when(i + AHEAD < PAIRS)
        def _():
            load(i + AHEAD).start()

        turn = (i + me) % 2
        for t in range(2):
            @pl.when(turn == t)
            def _():
                block(i, t, 3 * t)
                block(i, 1 - t, 1 + t)
        rows = pl.ds(pl.multiple_of(i * 32, 32), 32)
        for k in range(8):
            if late:
                out_ref[k, rows, :] = words[k * 32:k * 32 + 32, :]
            else:
                col = (me + k) % 8
                outs[k][rows, :] = words[pl.ds(pl.multiple_of(col * 32, 32), 32), :]
        return carry

    lax.fori_loop(0, PAIRS, pair, 0)


def moved(late, spectrum, sea, *edges):
    whole = pl.BlockSpec(memory_space=pltpu.VMEM)
    anywhere = pl.BlockSpec(memory_space=pl.ANY)
    rows = PAIRS * 32
    if late:
        out_shape, out_specs = jax.ShapeDtypeStruct((8, rows, 128), jnp.int32), whole
    else:
        out_shape = (jax.ShapeDtypeStruct((rows, 128), jnp.int32),) * 8
        out_shape += (jax.ShapeDtypeStruct((PAIRS * 8, NY), jnp.int32),) * 2
        out_specs = [whole] * 10
    return pl.pallas_call(
        functools.partial(move_kernel, late),
        in_specs=[anywhere] * 2 + [whole] * len(edges),
        out_specs=out_specs,
        out_shape=out_shape,
        scratch_shapes=[
            pltpu.VMEM((PAIRS, 16, COLS * NY), jnp.float32),
            pltpu.VMEM((1, COLS * NY), jnp.int32),
            pltpu.VMEM((COLS, 8, NY), jnp.float32),
            pltpu.VMEM((COLS, 8, NY), jnp.float32),
            pltpu.VMEM((COLS * 32, 128), jnp.int32),
            pltpu.SemaphoreType.DMA((PAIRS,)),
            pltpu.SemaphoreType.DMA,
        ],
        compiler_params=pltpu.CompilerParams(vmem_limit_bytes=(24 << 20) if late else LIMIT),
        name="move",
    )(spectrum, sea, *edges)


LIMIT = 59600 << 10


def pair_kernel(a_ref, b_ref, c_ref, d_ref, out_ref):
    for n, (one, two) in enumerate(((a_ref, b_ref), (c_ref, d_ref))):
        for g in range(GROUPS_F):
            a, b = one[g * 32:g * 32 + 32, :], two[g * 32:g * 32 + 32, :]
            at = (n * GROUPS_F + g) * 64
            out_ref[at:at + 32, :] = jnp.concatenate([a[:, :64], b[:, :64]], axis=1)
            out_ref[at + 32:at + 64, :] = jnp.concatenate([a[:, 64:], b[:, 64:]], axis=1)


def paired(tables):
    whole = pl.BlockSpec(memory_space=pltpu.VMEM)
    return pl.pallas_call(
        pair_kernel,
        in_specs=[whole] * 4,
        out_specs=whole,
        out_shape=jax.ShapeDtypeStruct((4 * GROUPS_F * 32, 128), jnp.bfloat16),
        compiler_params=pltpu.CompilerParams(vmem_limit_bytes=4 << 20),
        name="pair",
    )(*tables)


MARKS = ((2560, 128), jnp.bfloat16)
VALUES = ((320, 128), jnp.float32)


STASH = 32 + 2 * PAIRS * 32


def prepare_kernel(speed_ref, direction_ref, point_ref, route_ref, own_ref, out_ref, stash, sem):
    speed, direction = speed_ref[...], direction_ref[...]
    stash[0:8, :] = speed * jnp.cos(direction)
    stash[8:16, :] = speed * jnp.sin(direction)
    for at, ref in ((16, point_ref), (24, route_ref)):
        row = jnp.concatenate([ref[0:1, :]] * 2, axis=1).astype(jnp.float32)
        stash[at:at + 8, :] = jnp.broadcast_to(row, (8, 128))
    stash[32:32 + PAIRS * 32, :] = decode(low(own_ref[...]))
    stash[32 + PAIRS * 32:, :] = decode(high(own_ref[...]))
    copy = pltpu.make_async_copy(stash, out_ref.at[pl.ds(0, STASH), pl.ds(0, 128)], sem)
    copy.start()
    copy.wait()


def prepared(*operands):
    whole = pl.BlockSpec(memory_space=pltpu.VMEM)
    return pl.pallas_call(
        prepare_kernel,
        in_specs=[whole] * 5,
        out_specs=pl.BlockSpec(memory_space=pl.ANY),
        out_shape=jax.ShapeDtypeStruct((NC, NY), jnp.float32),
        scratch_shapes=[pltpu.VMEM((STASH, 128), jnp.float32), pltpu.SemaphoreType.DMA],
        compiler_params=pltpu.CompilerParams(vmem_limit_bytes=8 << 20),
        name="prepare",
    )(*operands)


def tabulate(stash, marks, values):
    tile = lax.axis_index("tile")
    x, y, core = tile // 8, (tile // 2) % 4, tile % 2
    route = jnp.broadcast_to(stash[24:25, :].astype(jnp.int32), (16, 128))
    for n in range(FARMS):
        farm = ((x - n % 4 + 4) % 4) * 8 + ((y - (n // 4) % 4 + 4) % 4) * 2 + (core + n // 16) % 2
        marks[2048 + 16 * n:2064 + 16 * n, :] = (route == farm).astype(jnp.float32).astype(jnp.bfloat16)
    slot_of = jnp.broadcast_to(stash[16:17, :].astype(jnp.int32), (128, 128))
    point_t = jnp.transpose(slot_of)
    for k in range(8):
        hit = lax.broadcasted_iota(jnp.int32, (128, 128), 0) + k * 128 == slot_of
        marks[128 * k:128 * k + 128, :] = hit.astype(jnp.float32).astype(jnp.bfloat16)
        hit = (lax.broadcasted_iota(jnp.int32, (128, 128), 1) + k * 128 == point_t).astype(jnp.float32)
        marks[1024 + 128 * k:1152 + 128 * k, :] = hit.astype(jnp.bfloat16)
        values[256 + 8 * k:264 + 8 * k, :] = jnp.broadcast_to(jnp.sum(hit, axis=0, keepdims=True), (8, 128))
    for d in range(ND):
        values[8 * d:8 * d + 8, :] = jnp.maximum(COS[d] * stash[0:8, :] + SIN[d] * stash[8:16, :], 0.0)


def finish_kernel(plus_hbm, minus_hbm, *rest):
    arrived = rest[:7]
    late, mine_ref, other_ref = rest[7:10]
    tables = (mine_ref, other_ref)
    out_ref, field, scr_a, scr_b, buf, stash, marks, values = rest[11:19]
    early = rest[19:26]
    plus_ref, minus_ref, sem, row_sems = rest[26:]
    corner = out_ref.at[pl.ds(0, STASH), pl.ds(0, 128)]
    loads = [pltpu.make_async_copy(src, dst, row_sems.at[2 + n])
             for n, (src, dst) in enumerate(zip((corner, *arrived), (stash, *early)))]
    for load in loads:
        load.start()
    me = lax.axis_index("comp")
    left_lanes = lax.broadcasted_iota(jnp.int32, (32, 128), 1) < 64
    upper = lax.broadcasted_iota(jnp.int32, (8, 128), 0) < 4
    rows_in = [pltpu.make_async_copy(plus_hbm, plus_ref, row_sems.at[0]),
               pltpu.make_async_copy(minus_hbm, minus_ref, row_sems.at[1])]
    for copy in rows_in:
        copy.start()

    going = jnp.where(me >= 2, 0, 1)

    def unpack(first_of, i, sums):
        low_sum, high_sum = list(sums[:4]), list(sums[4:])

        def halves_of(at, src, other):
            first = src * 144 + 16 * i + 8 * ((i + src + other) % 2)
            for v in range(4):
                a, b = at(i * 32 + v * 8)
                row = pl.multiple_of((first + 2 * v) * 8, 8)
                field[pl.ds(row, 8), :] = jnp.where(upper, a, pltpu.roll(b, 4, 0))
                field[pl.ds(row + 8, 8), :] = jnp.where(upper, pltpu.roll(a, 4, 0), b)
                low_sum[v] = low_sum[v] + a
                high_sum[v] = high_sum[v] + b

        def own_at(row):
            return (stash[pl.ds(pl.multiple_of(32 + row, 8), 8), :],
                    stash[pl.ds(pl.multiple_of(32 + PAIRS * 32 + row, 8), 8), :])

        def late_at(k, row):
            w = late[k, pl.ds(pl.multiple_of(row, 8), 8), :]
            return decode(low(w)), decode(high(w))

        def early_at(k, row):
            w = early[k - 1][pl.ds(pl.multiple_of(row, 8), 8), :]
            return decode(low(w)), decode(high(w))

        for k in range(8):
            if first_of:
                halves_of(functools.partial(late_at, k), k, 1 - going)
            elif k == 0:
                halves_of(own_at, me, going)
            else:
                halves_of(functools.partial(early_at, k), (me - k + 8) % 8, going)
        return tuple(low_sum + high_sum)

    sums = (jnp.zeros((8, 128), jnp.float32),) * 8
    sums = lax.fori_loop(0, PAIRS, functools.partial(unpack, True), sums)
    for load in loads:
        load.wait()
    tabulate(stash, marks, values)
    sums = lax.fori_loop(0, PAIRS, functools.partial(unpack, False), sums)
    lows, highs = (sums[0] + sums[1]) + (sums[2] + sums[3]), (sums[4] + sums[5]) + (sums[6] + sums[7])
    mean = jnp.where(upper, lows + pltpu.roll(lows, 4, 0), highs + pltpu.roll(highs, 4, 0)) * (break_rate / NC)
    for copy in rows_in:
        copy.wait()

    def source(g, scr):
        for j in range(4):
            f = g * 4 + j
            base = 1.0 - mean * (0.5 + f / NF)
            gain = (f + 1.0) * (grow_rate / NF)
            for d in range(ND):
                c = f * ND + d
                here = field[c * 8:c * 8 + 8, :]
                a = field[pl.ds(pl.multiple_of(plus_ref[c], 8), 8), :]
                b = field[pl.ds(pl.multiple_of(minus_ref[c], 8), 8), :]
                value = here * (base + gain * values[d * 8:d * 8 + 8, :]
                                + (pair_rate * here) * (a + b) - (2.0 * pair_rate) * (a * b))
                local = j * ND + d
                scr[local * 8:local * 8 + 8, :] = value

    def farm(g, scr):
        def cut(cb, k):
            return scr[pl.ds(cb * 64 + k, 8, stride=8), :]

        cells = jnp.zeros((128, 128), jnp.float32)
        for k in range(0, 8, 2):
            xk = [jnp.concatenate([cut(cb, kk) for cb in range(16)], axis=0).astype(jnp.bfloat16) for kk in (k, k + 1)]
            cells = cells + jnp.dot(jnp.concatenate(xk, axis=1), marks[k * 128:(k + 2) * 128, :],
                                    preferred_element_type=jnp.float32)
        both = []
        for p in range(2):
            rows = [cells[64 * p:64 * p + 32, :], cells[64 * p + 32:64 * p + 64, :]]
            own = jnp.concatenate([jnp.where(left_lanes, rows[0], 0.0), jnp.where(left_lanes, 0.0, rows[1])], axis=0)
            own = own.astype(jnp.bfloat16)
            farmed = jnp.zeros((32, 128), jnp.float32)
            for n in range(8):
                left = []
                for m in (2 * n, 2 * n + 1):
                    at = (m % 8 * GROUPS_F + g) * 64 + 32 * p
                    left.append(tables[m // 8][at:at + 32, :])
                right = [own * jnp.concatenate([marks[2048 + 16 * m:2064 + 16 * m, :]] * 4, axis=0)
                         for m in range(4 * n, 4 * n + 4)]
                farmed = farmed + jnp.dot(jnp.concatenate(left, axis=1), jnp.concatenate(right, axis=0),
                                          preferred_element_type=jnp.float32)
            top = farmed.astype(jnp.bfloat16).astype(jnp.float32)
            rest_of = farmed - top
            both.append(jnp.where(left_lanes, top, pltpu.roll(rest_of, 64, 1)).astype(jnp.bfloat16))
            both.append(jnp.where(left_lanes, pltpu.roll(top, 64, 1), rest_of).astype(jnp.bfloat16))
        both = jnp.concatenate(both, axis=0)
        for k in range(0, 8, 2):
            slots = jnp.concatenate([marks[1024 + 128 * kk:1152 + 128 * kk, :] for kk in (k, k + 1)], axis=1)
            spread = jnp.dot(both, slots, preferred_element_type=jnp.float32)
            for kk in range(2):
                at = slice((k + kk) * 128, (k + kk + 1) * 128)
                on = values[256 + 8 * (k + kk):264 + 8 * (k + kk), :] > 0.5
                for cb in range(16):
                    row = slice(g * 128 + cb * 8, g * 128 + cb * 8 + 8)
                    buf[row, at] = jnp.where(on, spread[cb * 8:cb * 8 + 8, kk * 128:(kk + 1) * 128], cut(cb, k + kk))

    def store(g):
        rows = pl.ds(g * 128, 128)
        pltpu.make_async_copy(buf.at[rows, :], out_ref.at[rows, :], sem).start()

    source(0, scr_a)
    for g in range(GROUPS_F - 1):
        here, there = (scr_a, scr_b) if g % 2 == 0 else (scr_b, scr_a)
        source(g + 1, there)
        farm(g, here)
        store(g)
    farm(GROUPS_F - 1, scr_a)
    store(GROUPS_F - 1)
    pltpu.make_async_copy(buf, out_ref, sem).wait()


def finished(plus, minus, pieces, second, mine, other, corner):
    whole = pl.BlockSpec(memory_space=pltpu.VMEM)
    anywhere = pl.BlockSpec(memory_space=pl.ANY)
    return pl.pallas_call(
        finish_kernel,
        in_specs=[anywhere] * 9 + [whole] * 3 + [anywhere],
        out_specs=anywhere,
        out_shape=jax.ShapeDtypeStruct((NC, NY), jnp.float32),
        input_output_aliases={12: 0},
        scratch_shapes=[
            pltpu.VMEM((NC * 8, 128), jnp.float32),
            pltpu.VMEM((1024, 128), jnp.float32),
            pltpu.VMEM((1024, 128), jnp.float32),
            pltpu.VMEM((NC, NY), jnp.float32),
            pltpu.VMEM((STASH, 128), jnp.float32),
            pltpu.VMEM(*MARKS),
            pltpu.VMEM(*VALUES),
            *[pltpu.VMEM((PAIRS * 32, 128), jnp.int32)] * 7,
            pltpu.SMEM((NC,), jnp.int32),
            pltpu.SMEM((NC,), jnp.int32),
            pltpu.SemaphoreType.DMA,
            pltpu.SemaphoreType.DMA((10,)),
        ],
        compiler_params=pltpu.CompilerParams(vmem_limit_bytes=28 << 20),
        name="finish",
    )(plus, minus, *pieces, second, mine, other, corner)


def after(value, *others):
    return lax.optimization_barrier((value,) + others)[0]


def local(spectrum, sea_mask, wind_speed, wind_dir, dia_plus, dia_minus, farm_point, farm_route, farm_matrix):
    tiles, comps = lax.axis_size("tile"), lax.axis_size("comp")
    sea = sea_mask.reshape(1, -1)
    up = [(i, i + 1) for i in range(tiles - 1)]
    down = [(i + 1, i) for i in range(tiles - 1)]
    *out, right, left = moved(False, spectrum, sea)
    west = lax.ppermute(right, "tile", up)
    east = lax.ppermute(left, "tile", down)
    pieces = []
    for k in range(1, comps):
        pieces.append(lax.ppermute(out[k], "comp", [(i, (i + k) % comps) for i in range(comps)]))

    def shift(dx, dy, dc):
        return [(x * 8 + y * 2 + c, ((x + dx) % 4) * 8 + ((y + dy) % 4) * 2 + (c ^ dc))
                for x in range(4) for y in range(4) for c in range(2)]

    def spread(value, axis):
        parts = [value]
        for k in (1, 2, 3):
            parts.append(lax.ppermute(value, "tile", shift(k, 0, 0) if axis == "x" else shift(0, k, 0)))
        return parts

    table = after(farm_matrix, right)[0]
    table = table.reshape(GROUPS_F, 4, ND, ND).transpose(0, 2, 1, 3).reshape(GROUPS_F * ND, 128)
    mine = jnp.concatenate(spread(paired(spread(table, "x")), "y"), axis=0)
    other = lax.ppermute(mine, "tile", shift(0, 0, 1))

    second = moved(True, spectrum, sea, west, east)
    second = lax.all_to_all(second, "comp", split_axis=0, concat_axis=0, tiled=True)

    plus, minus = after((dia_plus, dia_minus), out[1])
    corner = prepared(wind_speed.reshape(8, 128), wind_dir.reshape(8, 128), farm_point.reshape(1, SLOTS),
                      farm_route.reshape(1, SLOTS), out[0])
    return finished(plus * 8, minus * 8, pieces, second, mine, other, corner)


def solution(mesh):
    return jax.shard_map(
        local,
        mesh=mesh,
        in_specs=(
            P("comp", "tile"),
            P("tile"),
            P(("tile", "comp")),
            P(("tile", "comp")),
            P(),
            P(),
            P("tile", "comp", None),
            P("tile", "comp", None, None),
            P("tile", None, None, None),
        ),
        out_specs=P(None, ("tile", "comp")),
        check_vma=False,
    )
```
